256 devices in a mesh: gx: 16 (over x_hi, z), gy: 4 (over y), gz: 4 (over x_lo, core).
Axes of the slice: x: 4 (x_hi: 2, x_lo: 2; x = x_hi * 2 + x_lo), y: 4, z: 8, core: 2. Of those that a mesh axis runs over, the one named last changes fastest.
Arguments:
- scalar_field: float32 [64, 1536, 1536], P('gx', 'gy', 'gz'), may hold values from 0 to 1
- materials: int32 [64, 1536, 1536], P('gx', 'gy', 'gz'), may hold values from 0 to 7
- transfer_table: float32 [4, 128], replicated, may hold values from 0.1 to 3
- material_gain: float32 [4, 8], replicated, may hold values from 0.3 to 3
- depth_order_x: int32 [4, 4, 16], replicated, may hold values from 0 to 15, each once within a row
- depth_order_y: int32 [4], replicated, may hold values from 0 to 3, each once
- depth_order_z: int32 [4], replicated, may hold values from 0 to 3, each once
Outputs:
- frame_along_x: float32 [4, 4, 16, 24, 1536], P(None, 'gy', 'gx', None, 'gz')
- frame_along_y: float32 [4, 64, 1536], P(None, 'gx', 'gz')
- frame_along_z: float32 [4, 64, 1536], P(None, 'gx', 'gy')
The draws below stay inside these ranges and needn't reach their ends.
Inputs may be any that keep to these rules, and one draw needn't show every extreme that they name: `depth_order_x`: entry [a, b, k] names the x slab that lies k-th from the viewer in the frame tile of y slab a and z slab b; every slab once in each tile. `depth_order_y`: entry k names the slab that lies k-th from the viewer; every slab once. `depth_order_z`: entry k names the slab that lies k-th from the viewer; every slab once.
All inputs are finite; a program needn't handle non-finite values.
Results may differ from the reference program's by a relative error of at most 0.0003.
Values sent between devices are 32-bit elements; how exact they have to be, the bound alone decides.
No kernel may reach another device: no remote copies, remote signals or barrier semaphores. Data moves between devices by JAX's collectives and lax.ppermute only.
A program may use at most 128 MiB of HBM per device.

```python
import math
import jax
import jax.numpy as jnp
from jax import lax

CX = 4
CY = 384
CZ = 384
TF_BINS = 128
MATS = 8
NX = 64
NY = 1536
NZ = 1536
N_GX = 16
N_GY = 4
N_GZ = 4


def plant(array, key, least, largest):
    longest = array.shape.index(max(array.shape))
    spots = []
    for shift in (0, 1):
        where = [jax.random.randint(jax.random.fold_in(key, axis), (), 0, length) for axis, length in enumerate(array.shape)]
        where[longest] = (where[longest] + shift) % array.shape[longest]
        spots.append(tuple(where))
    return array.at[spots[0]].set(least).at[spots[1]].set(largest)


def level_of(rng, shape, pieces, low, largest):
    level = 1.0
    for axis_at, parts in pieces:
        draws = jax.random.uniform(jax.random.fold_in(jax.random.fold_in(rng, 6), axis_at), (parts,), jnp.float32, low / len(pieces), largest / len(pieces))
        level = level * jnp.repeat(jnp.exp(draws), shape[axis_at] // parts).reshape((-1,) + (1,) * (len(shape) - 1 - axis_at))
    return level


def setup_inputs(seed: int = 0) -> dict:
    seeds = jax.random.split(jax.random.key(seed), 8)
    return {
        "scalar_field": jnp.clip(1.0 * jax.random.uniform(seeds[0], (NX, NY, NZ), jnp.float32) ** level_of(seeds[0], (NX, NY, NZ), ((0, 16), (1, 4), (2, 4)), -0.2, 0.2), 0.0, 1.0),
        "materials": plant(jax.random.randint(seeds[1], (NX, NY, NZ), 0, MATS), jax.random.fold_in(seeds[1], 1), 0, MATS - 1).astype(jnp.int32),
        "transfer_table": jnp.clip(jax.random.uniform(seeds[2], (4, TF_BINS), jnp.float32, 0.1, 3.0), 0.1, 3.0),
        "material_gain": jnp.clip(jnp.exp(jax.random.uniform(seeds[3], (4, MATS), jnp.float32, math.log(0.3), math.log(3.0))), 0.3, 3.0),
        "depth_order_x": jax.vmap(lambda own: jax.random.permutation(own, N_GX))(jax.random.split(seeds[4], N_GY * N_GZ)).reshape((N_GY, N_GZ, N_GX)).astype(jnp.int32),
        "depth_order_y": jax.random.permutation(seeds[5], N_GY).astype(jnp.int32),
        "depth_order_z": jax.random.permutation(seeds[6], N_GZ).astype(jnp.int32),
    }


def classify_cells(cube, marks, transfer_table, material_gain):
    bin_count = transfer_table.shape[1]
    scaled = cube * (bin_count - 1.0)
    lower = jnp.clip(jnp.floor(scaled), 0.0, bin_count - 2.0)
    fraction = scaled - lower
    position = lower.astype(jnp.int32)
    sample = transfer_table[:, position] * (1.0 - fraction) + transfer_table[:, position + 1] * fraction
    return sample * material_gain[:, marks]


def march(classes, march_dim, step_size):
    emission = classes[0:3]
    extinction = classes[3]
    before = jnp.cumsum(extinction, axis=march_dim) - extinction
    opacity = 1.0 - jnp.exp(-step_size * extinction)
    weights = jnp.exp(-step_size * before) * opacity
    colour = jnp.sum(weights[None] * emission, axis=march_dim + 1)
    through = jnp.exp(-step_size * jnp.sum(extinction, axis=march_dim))
    return jnp.concatenate([colour, through[None]], axis=0)


def composite(slab_list, depth_order):
    ranked = jnp.take(slab_list, depth_order, axis=0)
    through = ranked[:, 3]
    front_side = jnp.cumprod(through, axis=0)
    before = jnp.concatenate([jnp.ones_like(front_side[:1]), front_side[:-1]], axis=0)
    colour = jnp.sum(before[:, None] * ranked[:, 0:3], axis=0)
    return jnp.concatenate([colour, front_side[-1][None]], axis=0)


def reference(scalar_field, materials, transfer_table, material_gain, depth_order_x, depth_order_y, depth_order_z):
    step_x = 1.0 / (CX * N_GX)
    step_y = 1.0 / (CY * N_GY)
    step_z = 1.0 / (CZ * N_GZ)

    def one_brick(number):
        first = number // (N_GY * N_GZ)
        second = (number // N_GZ) % N_GY
        third = number % N_GZ
        starts = ((first * CX).astype(jnp.int32), (second * CY).astype(jnp.int32), (third * CZ).astype(jnp.int32))
        cube = lax.dynamic_slice(scalar_field, starts, (CX, CY, CZ))
        marks = lax.dynamic_slice(materials, starts, (CX, CY, CZ))
        classes = classify_cells(cube, marks, transfer_table, material_gain)
        return march(classes, 0, step_x), march(classes, 1, step_y), march(classes, 2, step_z)

    numbers = jnp.arange(N_GX * N_GY * N_GZ, dtype=jnp.int32)
    part_x, part_y, part_z = lax.map(one_brick, numbers)
    tiles_x = part_x.reshape(N_GX, N_GY, N_GZ, 4, CY, CZ)
    slabs_y = part_y.reshape(N_GX, N_GY, N_GZ, 4, CX, CZ).transpose(1, 3, 0, 4, 2, 5).reshape(N_GY, 4, N_GX * CX, N_GZ * CZ)
    slabs_z = part_z.reshape(N_GX, N_GY, N_GZ, 4, CX, CY).transpose(2, 3, 0, 4, 1, 5).reshape(N_GZ, 4, N_GX * CX, N_GY * CY)
    rows_list = []
    for band in range(N_GY):
        cols_list = []
        for column in range(N_GZ):
            cols_list.append(composite(tiles_x[:, band, column], depth_order_x[band, column]))
        rows_list.append(jnp.concatenate(cols_list, axis=2))
    whole_x = jnp.concatenate(rows_list, axis=1)
    frame_along_x = whole_x.reshape(4, N_GY, N_GX, CY // N_GX, N_GZ * CZ)
    frame_along_y = composite(slabs_y, depth_order_y)
    frame_along_z = composite(slabs_z, depth_order_z)
    return frame_along_x, frame_along_y, frame_along_z
```

```python
import functools, math
import jax
import jax.numpy as jnp
from jax import lax
from jax.experimental import pallas as pl
from jax.experimental.pallas import tpu as pltpu
from jax.sharding import PartitionSpec as P

LOG2E = math.log2(math.e)


def look_up(table, index):
    return jnp.take_along_axis(table, index, axis=1, mode="promise_in_bounds")


def make_tables(transfer_ref, tables_ref):
    bins = transfer_ref.shape[1]
    lane = lax.broadcasted_iota(jnp.int32, (8, 128), 1)
    for c in range(4):
        value = jnp.broadcast_to(transfer_ref[pl.ds(c, 1), :], (8, bins))
        tables_ref[c] = value
        tables_ref[4 + c] = jnp.where(lane == bins - 1, 0.0, pltpu.roll(value, bins - 1, 1) - value)


def classify(cells, marks, tables, gain_ref):
    scaled = cells * (tables[0].shape[1] - 1.0)
    lower = scaled.astype(jnp.int32)
    fraction = scaled - lower.astype(jnp.float32)
    values = [look_up(tables[c], lower) for c in range(4)]
    slopes = [look_up(tables[4 + c], lower) for c in range(4)]
    bits = [marks & (1 << k) != 0 for k in range((gain_ref.shape[1] - 1).bit_length())]
    out = []
    for c in range(4):
        gains = [gain_ref[c, k] for k in range(gain_ref.shape[1])]
        for bit in bits:
            gains = [jnp.where(bit, high, low) for low, high in zip(gains[0::2], gains[1::2])]
        out.append((values[c] + fraction * slopes[c]) * gains[0])
    return out


def x_kernel(step, field_ref, mark_ref, transfer_ref, gain_ref, out_ref, tables_ref):
    @pl.when(pl.program_id(0) == 0)
    def _():
        make_tables(transfer_ref, tables_ref)

    tables = [tables_ref[k] for k in range(8)]
    depth, rows, cols = field_ref.shape
    piece_rows = out_ref.shape[2]
    for piece in range(out_ref.shape[0]):
        for col in range(0, cols, 128):
            for row in range(0, piece_rows, 8):
                colour = None
                for x in range(depth):
                    at = (x, pl.ds(piece * piece_rows + row, 8), pl.ds(col, 128))
                    red, green, blue, extinction = classify(field_ref[at], mark_ref[at], tables, gain_ref)
                    passed = jnp.exp(extinction * -step)
                    opacity = 1.0 - passed
                    if colour is None:
                        colour = [opacity * v for v in (red, green, blue)]
                        through = passed
                    else:
                        weight = through * opacity
                        colour = [a + weight * v for a, v in zip(colour, (red, green, blue))]
                        through = through * passed
                for c, v in enumerate(colour + [through]):
                    out_ref[piece, c, pl.ds(row, 8), pl.ds(col, 128)] = v


def x_view(field, marks, transfer_table, material_gain, step, pieces, per_step=4):
    depth, rows, cols = field.shape
    piece_rows = rows // pieces
    block = pl.BlockSpec((depth, per_step * piece_rows, cols), lambda i: (0, i, 0))
    return pl.pallas_call(
        functools.partial(x_kernel, step),
        grid=(pieces // per_step,),
        in_specs=[
            block,
            block,
            pl.BlockSpec(transfer_table.shape, lambda i: (0, 0)),
            pl.BlockSpec(memory_space=pltpu.SMEM),
        ],
        out_specs=pl.BlockSpec((per_step, 4, piece_rows, cols), lambda i: (i, 0, 0, 0)),
        out_shape=jax.ShapeDtypeStruct((pieces, 4, piece_rows, cols), jnp.float32),
        scratch_shapes=[pltpu.VMEM((8, 8, 128), jnp.float32)],
        name="x_view",
    )(field, marks, transfer_table, material_gain)


def join_rows(colour, through):
    total = [v[0:1] for v in colour]
    front = through[0:1]
    for s in range(1, 8):
        total = [t + front * v[s : s + 1] for t, v in zip(total, colour)]
        front = front * through[s : s + 1]
    return total + [front]


def add_cell(state, passed, emission):
    red, green, blue, through = state
    weight = through * (1.0 - passed)
    return (
        red + weight * emission[0],
        green + weight * emission[1],
        blue + weight * emission[2],
        through * passed,
    )


def start_state():
    zero = jnp.zeros((8, 128), jnp.float32)
    return (zero, zero, zero, jnp.ones((8, 128), jnp.float32))


def yz_kernel(step, field_ref, mark_ref, transfer_ref, gain_ref, y_ref, z_ref, tables_ref, cell_ref, turned_ref):
    tile = pl.program_id(1)

    @pl.when((pl.program_id(0) == 0) & (tile == 0))
    def _():
        make_tables(transfer_ref, tables_ref)

    tables = [tables_ref[k] for k in range(8)]
    rows = field_ref.shape[1]
    run = rows // 8

    def along_y(j, state):
        at = pl.ds(j, 8, stride=run)
        red, green, blue, extinction = classify(field_ref[0, at, :], mark_ref[0, at, :], tables, gain_ref)
        passed = jnp.exp(extinction * -step)
        for c, v in enumerate((red, green, blue, passed)):
            cell_ref[c, at, :] = v
        return add_cell(state, passed, (red, green, blue))

    state = lax.fori_loop(0, run, along_y, start_state(), unroll=16)
    for c, v in enumerate(join_rows(state[:3], state[3])):
        y_ref[0, c, :] = v[0]

    to = pl.ds(pl.multiple_of(tile * 128, 128), 128)
    for c in range(4):
        for k in range(rows // 128):
            turned_ref[c, k, to, :] = cell_ref[c, pl.ds(k * 128, 128), :].T

    @pl.when(tile == pl.num_programs(1) - 1)
    def _():
        length = turned_ref.shape[2]
        run = length // 8
        for k in range(turned_ref.shape[1]):

            def along_z(j, state):
                at = pl.ds(j, 8, stride=run)
                red, green, blue, passed = [turned_ref[c, k, at, :] for c in range(4)]
                return add_cell(state, passed, (red, green, blue))

            state = lax.fori_loop(0, run, along_z, start_state(), unroll=8)
            for c, v in enumerate(join_rows(state[:3], state[3])):
                z_ref[0, c, pl.ds(k * 128, 128)] = v[0]


def yz_views(field, marks, transfer_table, material_gain, step):
    depth, rows, cols = field.shape
    block = pl.BlockSpec((1, rows, 128), lambda i, j: (i, 0, j))
    return pl.pallas_call(
        functools.partial(yz_kernel, step),
        grid=(depth, cols // 128),
        in_specs=[
            block,
            block,
            pl.BlockSpec(transfer_table.shape, lambda i, j: (0, 0)),
            pl.BlockSpec(memory_space=pltpu.SMEM),
        ],
        out_specs=[
            pl.BlockSpec((1, 4, 128), lambda i, j: (i, 0, j)),
            pl.BlockSpec((1, 4, rows), lambda i, j: (i, 0, 0)),
        ],
        out_shape=[
            jax.ShapeDtypeStruct((depth, 4, cols), jnp.float32),
            jax.ShapeDtypeStruct((depth, 4, rows), jnp.float32),
        ],
        scratch_shapes=[
            pltpu.VMEM((8, 8, 128), jnp.float32),
            pltpu.VMEM((4, rows, 128), jnp.float32),
            pltpu.VMEM((4, rows // 128, cols, 128), jnp.float32),
        ],
        name="yz_views",
    )(field, marks, transfer_table, material_gain)


def x_frame_kernel(order_ref, part_ref, out_ref):
    slabs = part_ref.shape[0]
    first = part_ref.at[order_ref[0]]
    total = [first[c] for c in range(3)]
    front = first[3]
    for k in range(1, slabs):
        part = part_ref.at[order_ref[k]]
        total = [t + front * part[c] for c, t in enumerate(total)]
        front = front * part[3]
    for c, v in enumerate(total + [front]):
        out_ref[c] = v


def x_frame(parts, order):
    return pl.pallas_call(
        x_frame_kernel,
        in_specs=[pl.BlockSpec(memory_space=pltpu.SMEM), pl.BlockSpec(memory_space=pltpu.VMEM)],
        out_specs=pl.BlockSpec(memory_space=pltpu.VMEM),
        out_shape=jax.ShapeDtypeStruct(parts.shape[1:], jnp.float32),
        name="x_frame",
    )(order, parts)


def yz_frame_kernel(y_order_ref, z_order_ref, y_part_ref, z_part_ref, y_out_ref, z_out_ref):
    for order_ref, part_ref, out_ref in (
        (y_order_ref, y_part_ref, y_out_ref),
        (z_order_ref, z_part_ref, z_out_ref),
    ):
        slabs, depth, _, cols = part_ref.shape
        for x in range(depth):
            first = part_ref.at[order_ref[0], x]
            total = [first[pl.ds(c, 1), :] for c in range(3)]
            front = first[pl.ds(3, 1), :]
            for k in range(1, slabs):
                part = part_ref.at[order_ref[k], x]
                total = [t + front * part[pl.ds(c, 1), :] for c, t in enumerate(total)]
                front = front * part[pl.ds(3, 1), :]
            for c, v in enumerate(total + [front]):
                out_ref[c, pl.ds(x, 1), :] = v


def yz_frames(y_parts, z_parts, y_order, z_order):
    smem = pl.BlockSpec(memory_space=pltpu.SMEM)
    vmem = pl.BlockSpec(memory_space=pltpu.VMEM)
    shape = lambda parts: jax.ShapeDtypeStruct((4, parts.shape[1], parts.shape[3]), jnp.float32)
    return pl.pallas_call(
        yz_frame_kernel,
        in_specs=[smem, smem, vmem, vmem],
        out_specs=[vmem, vmem],
        out_shape=[shape(y_parts), shape(z_parts)],
        name="yz_frames",
    )(y_order, z_order, y_parts, z_parts)


def shards(scalar_field, materials, transfer_table, material_gain, depth_order_x, depth_order_y, depth_order_z):
    cells_x, cells_y, cells_z = scalar_field.shape
    pieces = lax.axis_size("gx")
    step_x = 1.0 / (cells_x * pieces)
    step_y = 1.0 / (cells_y * lax.axis_size("gy"))
    step_z = 1.0 / (cells_z * lax.axis_size("gz"))
    assert step_y == step_z
    image_x = x_view(scalar_field, materials, transfer_table, material_gain, step_x, pieces)
    parts_x = lax.all_to_all(image_x, "gx", split_axis=0, concat_axis=0, tiled=True)
    image_y, image_z = yz_views(scalar_field, materials, transfer_table, material_gain, step_y)
    parts_y = lax.all_gather(image_y, "gy", axis=0)
    parts_z = lax.all_gather(image_z, "gz", axis=0)
    frame_y, frame_z = yz_frames(parts_y, parts_z, depth_order_y, depth_order_z)
    tile_order = depth_order_x[lax.axis_index("gy"), lax.axis_index("gz")]
    frame_x = x_frame(parts_x, tile_order)
    return frame_x[:, None, None], frame_y, frame_z


def solution(mesh):
    return jax.shard_map(
        shards,
        mesh=mesh,
        in_specs=(P("gx", "gy", "gz"), P("gx", "gy", "gz"), P(), P(), P(), P(), P()),
        out_specs=(P(None, "gy", "gx", None, "gz"), P(None, "gx", "gz"), P(None, "gx", "gy")),
        check_vma=False,
    )
```

```python
import functools
import jax
import jax.numpy as jnp
from jax import lax
from jax.experimental import pallas as pl
from jax.experimental.pallas import tpu as pltpu
from jax.sharding import PartitionSpec as P


def look_up(table, index):
    return jnp.take_along_axis(table, index, axis=1, mode="promise_in_bounds")


def make_tables(transfer_ref, tables_ref):
    bins = transfer_ref.shape[1]
    lane = lax.broadcasted_iota(jnp.int32, (8, 128), 1)
    for c in range(4):
        value = jnp.broadcast_to(transfer_ref[pl.ds(c, 1), :], (8, bins))
        tables_ref[c] = value
        tables_ref[4 + c] = jnp.where(lane == bins - 1, 0.0, pltpu.roll(value, bins - 1, 1) - value)


def classify(cells, marks, tables, gain_ref):
    scaled = cells * (tables[0].shape[1] - 1.0)
    lower = scaled.astype(jnp.int32)
    fraction = scaled - lower.astype(jnp.float32)
    values = [look_up(tables[c], lower) for c in range(4)]
    slopes = [look_up(tables[4 + c], lower) for c in range(4)]
    bits = [marks & (1 << k) != 0 for k in range((gain_ref.shape[1] - 1).bit_length())]
    out = []
    for c in range(4):
        gains = [gain_ref[c, k] for k in range(gain_ref.shape[1])]
        for bit in bits:
            gains = [jnp.where(bit, high, low) for low, high in zip(gains[0::2], gains[1::2])]
        out.append((values[c] + fraction * slopes[c]) * gains[0])
    return out


def x_kernel(step, field_ref, mark_ref, transfer_ref, gain_ref, out_ref, tables_ref):
    @pl.when(pl.program_id(0) == 0)
    def _():
        make_tables(transfer_ref, tables_ref)

    tables = [tables_ref[k] for k in range(8)]
    depth, rows, cols = field_ref.shape
    piece_rows = out_ref.shape[2]
    for piece in range(out_ref.shape[0]):
        for col in range(0, cols, 128):
            for row in range(0, piece_rows, 8):
                colour = None
                for x in range(depth):
                    at = (x, pl.ds(piece * piece_rows + row, 8), pl.ds(col, 128))
                    red, green, blue, extinction = classify(field_ref[at], mark_ref[at], tables, gain_ref)
                    passed = jnp.exp(extinction * -step)
                    opacity = 1.0 - passed
                    if colour is None:
                        colour = [opacity * v for v in (red, green, blue)]
                        through = passed
                    else:
                        weight = through * opacity
                        colour = [a + weight * v for a, v in zip(colour, (red, green, blue))]
                        through = through * passed
                for c, v in enumerate(colour + [through]):
                    out_ref[piece, c, pl.ds(row, 8), pl.ds(col, 128)] = v


def x_view(field, marks, transfer_table, material_gain, step, pieces, per_step=4):
    depth, rows, cols = field.shape
    piece_rows = rows // pieces
    block = pl.BlockSpec((depth, per_step * piece_rows, cols), lambda i: (0, i, 0))
    return pl.pallas_call(
        functools.partial(x_kernel, step),
        grid=(pieces // per_step,),
        in_specs=[
            block,
            block,
            pl.BlockSpec(transfer_table.shape, lambda i: (0, 0)),
            pl.BlockSpec(memory_space=pltpu.SMEM),
        ],
        out_specs=pl.BlockSpec((per_step, 4, piece_rows, cols), lambda i: (i, 0, 0, 0)),
        out_shape=jax.ShapeDtypeStruct((pieces, 4, piece_rows, cols), jnp.float32),
        scratch_shapes=[pltpu.VMEM((8, 8, 128), jnp.float32)],
        name="x_view",
    )(field, marks, transfer_table, material_gain)


def join_rows(colour, through):
    total = [v[0:1] for v in colour]
    front = through[0:1]
    for s in range(1, 8):
        total = [t + front * v[s : s + 1] for t, v in zip(total, colour)]
        front = front * through[s : s + 1]
    return total + [front]


def add_cell(state, passed, emission):
    red, green, blue, through = state
    weight = through * (1.0 - passed)
    return (
        red + weight * emission[0],
        green + weight * emission[1],
        blue + weight * emission[2],
        through * passed,
    )


def start_state():
    zero = jnp.zeros((8, 128), jnp.float32)
    return (zero, zero, zero, jnp.ones((8, 128), jnp.float32))


def yz_kernel(step, field_ref, mark_ref, transfer_ref, gain_ref, y_ref, z_ref, tables_ref, cell_ref, turned_ref):
    tile = pl.program_id(1)

    @pl.when((pl.program_id(0) == 0) & (tile == 0))
    def _():
        make_tables(transfer_ref, tables_ref)

    tables = [tables_ref[k] for k in range(8)]
    rows = field_ref.shape[1]
    run = rows // 8

    def along_y(j, state):
        at = pl.ds(j, 8, stride=run)
        red, green, blue, extinction = classify(field_ref[0, at, :], mark_ref[0, at, :], tables, gain_ref)
        passed = jnp.exp(extinction * -step)
        for c, v in enumerate((red, green, blue, passed)):
            cell_ref[c, at, :] = v
        return add_cell(state, passed, (red, green, blue))

    state = lax.fori_loop(0, run, along_y, start_state(), unroll=16)
    for c, v in enumerate(join_rows(state[:3], state[3])):
        y_ref[0, c, :] = v[0]

    to = pl.ds(pl.multiple_of(tile * 128, 128), 128)
    for c in range(4):
        for k in range(rows // 128):
            turned_ref[c, k, to, :] = cell_ref[c, pl.ds(k * 128, 128), :].T

    @pl.when(tile == pl.num_programs(1) - 1)
    def _():
        length = turned_ref.shape[2]
        run = length // 8
        for k in range(turned_ref.shape[1]):

            def along_z(j, state):
                at = pl.ds(j, 8, stride=run)
                red, green, blue, passed = [turned_ref[c, k, at, :] for c in range(4)]
                return add_cell(state, passed, (red, green, blue))

            state = lax.fori_loop(0, run, along_z, start_state(), unroll=8)
            for c, v in enumerate(join_rows(state[:3], state[3])):
                z_ref[0, c, pl.ds(k * 128, 128)] = v[0]


def yz_views(field, marks, transfer_table, material_gain, step):
    depth, rows, cols = field.shape
    block = pl.BlockSpec((1, rows, 128), lambda i, j: (i, 0, j))
    return pl.pallas_call(
        functools.partial(yz_kernel, step),
        grid=(depth, cols // 128),
        in_specs=[
            block,
            block,
            pl.BlockSpec(transfer_table.shape, lambda i, j: (0, 0)),
            pl.BlockSpec(memory_space=pltpu.SMEM),
        ],
        out_specs=[
            pl.BlockSpec((1, 4, 128), lambda i, j: (i, 0, j)),
            pl.BlockSpec((1, 4, rows), lambda i, j: (i, 0, 0)),
        ],
        out_shape=[
            jax.ShapeDtypeStruct((depth, 4, cols), jnp.float32),
            jax.ShapeDtypeStruct((depth, 4, rows), jnp.float32),
        ],
        scratch_shapes=[
            pltpu.VMEM((8, 8, 128), jnp.float32),
            pltpu.VMEM((4, rows, 128), jnp.float32),
            pltpu.VMEM((4, rows // 128, cols, 128), jnp.float32),
        ],
        name="yz_views",
    )(field, marks, transfer_table, material_gain)


def x_frame_kernel(order_ref, part_ref, out_ref):
    slabs = part_ref.shape[0]
    first = part_ref.at[order_ref[0]]
    total = [first[c] for c in range(3)]
    front = first[3]
    for k in range(1, slabs):
        part = part_ref.at[order_ref[k]]
        total = [t + front * part[c] for c, t in enumerate(total)]
        front = front * part[3]
    for c, v in enumerate(total + [front]):
        out_ref[c] = v


def x_frame(parts, order):
    return pl.pallas_call(
        x_frame_kernel,
        in_specs=[pl.BlockSpec(memory_space=pltpu.SMEM), pl.BlockSpec(memory_space=pltpu.VMEM)],
        out_specs=pl.BlockSpec(memory_space=pltpu.VMEM),
        out_shape=jax.ShapeDtypeStruct(parts.shape[1:], jnp.float32),
        compiler_params=pltpu.CompilerParams(vmem_limit_bytes=8 << 20),
        name="x_frame",
    )(order, parts)


def yz_frame_kernel(y_order_ref, z_order_ref, y_part_ref, z_part_ref, y_out_ref, z_out_ref):
    for order_ref, part_ref, out_ref in (
        (y_order_ref, y_part_ref, y_out_ref),
        (z_order_ref, z_part_ref, z_out_ref),
    ):
        slabs, depth, _, cols = part_ref.shape
        for x in range(depth):
            first = part_ref.at[order_ref[0], x]
            total = [first[pl.ds(c, 1), :] for c in range(3)]
            front = first[pl.ds(3, 1), :]
            for k in range(1, slabs):
                part = part_ref.at[order_ref[k], x]
                total = [t + front * part[pl.ds(c, 1), :] for c, t in enumerate(total)]
                front = front * part[pl.ds(3, 1), :]
            for c, v in enumerate(total + [front]):
                out_ref[c, pl.ds(x, 1), :] = v


def yz_frames(y_parts, z_parts, y_order, z_order):
    smem = pl.BlockSpec(memory_space=pltpu.SMEM)
    vmem = pl.BlockSpec(memory_space=pltpu.VMEM)
    shape = lambda parts: jax.ShapeDtypeStruct((4, parts.shape[1], parts.shape[3]), jnp.float32)
    return pl.pallas_call(
        yz_frame_kernel,
        in_specs=[smem, smem, vmem, vmem],
        out_specs=[vmem, vmem],
        out_shape=[shape(y_parts), shape(z_parts)],
        name="yz_frames",
    )(y_order, z_order, y_parts, z_parts)


def shards(scalar_field, materials, transfer_table, material_gain, depth_order_x, depth_order_y, depth_order_z):
    cells_x, cells_y, cells_z = scalar_field.shape
    pieces = lax.axis_size("gx")
    step_x = 1.0 / (cells_x * pieces)
    step_y = 1.0 / (cells_y * lax.axis_size("gy"))
    step_z = 1.0 / (cells_z * lax.axis_size("gz"))
    assert step_y == step_z
    image_x = x_view(scalar_field, materials, transfer_table, material_gain, step_x, pieces)
    parts_x = lax.all_to_all(image_x, "gx", split_axis=0, concat_axis=0, tiled=True)
    image_y, image_z = yz_views(scalar_field, materials, transfer_table, material_gain, step_y)
    parts_y = lax.all_gather(image_y, "gy", axis=0)
    parts_z = lax.all_gather(image_z, "gz", axis=0)
    frame_y, frame_z = yz_frames(parts_y, parts_z, depth_order_y, depth_order_z)
    tile_order = depth_order_x[lax.axis_index("gy"), lax.axis_index("gz")]
    frame_x = x_frame(parts_x, tile_order)
    return frame_x[:, None, None], frame_y, frame_z


def solution(mesh):
    return jax.shard_map(
        shards,
        mesh=mesh,
        in_specs=(P("gx", "gy", "gz"), P("gx", "gy", "gz"), P(), P(), P(), P(), P()),
        out_specs=(P(None, "gy", "gx", None, "gz"), P(None, "gx", "gz"), P(None, "gx", "gy")),
        check_vma=False,
    )
```

```python
import functools
import jax
import jax.numpy as jnp
from jax import lax
from jax.experimental import pallas as pl
from jax.experimental.pallas import tpu as pltpu
from jax.sharding import PartitionSpec as P


LOG2_E = 1.4426950408889634


def look_up(table, index):
    return jnp.take_along_axis(table, index, axis=1, mode="promise_in_bounds")


def make_tables(transfer_ref, tables_ref):
    bins = transfer_ref.shape[1]
    lane = lax.broadcasted_iota(jnp.int32, (8, 128), 1)
    values, steps = [], []
    for c in range(4):
        value = jnp.broadcast_to(transfer_ref[pl.ds(c, 1), :], (8, bins))
        step = jnp.where(lane == bins - 1, 0.0, pltpu.roll(value, bins - 1, 1) - value)
        values.append((value * float(1 << 19) - 0.5).astype(jnp.int32) << 10)
        steps.append((step * float(1 << 18) + 1048576.0).astype(jnp.int32) - 1048576)
    for pair in range(2):
        first, second = 2 * pair, 2 * pair + 1
        tables_ref[3 * pair] = values[first] | (steps[second] & 1023)
        tables_ref[3 * pair + 1] = values[second] | 512
        tables_ref[3 * pair + 2] = (steps[first] << 11) | ((steps[second] >> 10) & 2047)


def classify(cells, marks, tables, gain_ref, extinction_scale=1.0):
    scaled = cells * (tables[0].shape[1] - 1.0)
    lower = scaled.astype(jnp.int32)
    fraction = scaled - lower.astype(jnp.float32)
    words = [look_up(table, lower) for table in tables]
    samples = []
    for pair in range(2):
        first, second, step = words[3 * pair : 3 * pair + 3]
        samples.append(first.astype(jnp.float32) + fraction * step.astype(jnp.float32))
        step = (step << 21) | ((first & 1023) << 11)
        samples.append(second.astype(jnp.float32) + fraction * step.astype(jnp.float32))
    bits = [marks & (1 << k) != 0 for k in range((gain_ref.shape[1] - 1).bit_length())]
    out = []
    for c in range(4):
        scale = (extinction_scale if c == 3 else 1.0) / (1 << 29)
        gains = [gain_ref[c, k] * scale for k in range(gain_ref.shape[1])]
        for bit in bits:
            gains = [jnp.where(bit, high, low) for low, high in zip(gains[0::2], gains[1::2])]
        out.append(samples[c] * gains[0])
    return out


def x_kernel(step, field_ref, mark_ref, transfer_ref, gain_ref, out_ref, tables_ref):
    @pl.when(pl.program_id(0) == 0)
    def _():
        make_tables(transfer_ref, tables_ref)

    tables = [tables_ref[k] for k in range(6)]
    depth, rows, cols = field_ref.shape
    piece_rows = out_ref.shape[2]
    for piece in range(out_ref.shape[0]):
        for col in range(0, cols, 128):
            for row in range(0, piece_rows, 8):
                colour = None
                for x in range(depth):
                    at = (x, pl.ds(piece * piece_rows + row, 8), pl.ds(col, 128))
                    red, green, blue, extinction = classify(field_ref[at], mark_ref[at], tables, gain_ref, -step * LOG2_E)
                    passed = jnp.exp2(extinction)
                    if colour is None:
                        weight = 1.0 - passed
                        colour = [weight * v for v in (red, green, blue)]
                        through = passed
                    else:
                        after = through * passed
                        weight = through - after
                        colour = [a + weight * v for a, v in zip(colour, (red, green, blue))]
                        through = after
                for c, v in enumerate(colour + [through]):
                    out_ref[piece, c, pl.ds(row, 8), pl.ds(col, 128)] = v


def x_view(field, marks, transfer_table, material_gain, step, pieces, per_step=4):
    depth, rows, cols = field.shape
    piece_rows = rows // pieces
    block = pl.BlockSpec((depth, per_step * piece_rows, cols), lambda i: (0, i, 0))
    return pl.pallas_call(
        functools.partial(x_kernel, step),
        grid=(pieces // per_step,),
        in_specs=[
            block,
            block,
            pl.BlockSpec(transfer_table.shape, lambda i: (0, 0)),
            pl.BlockSpec(memory_space=pltpu.SMEM),
        ],
        out_specs=pl.BlockSpec((per_step, 4, piece_rows, cols), lambda i: (i, 0, 0, 0)),
        out_shape=jax.ShapeDtypeStruct((pieces, 4, piece_rows, cols), jnp.float32),
        scratch_shapes=[pltpu.VMEM((6, 8, 128), jnp.int32)],
        name="x_view",
    )(field, marks, transfer_table, material_gain)


def join_rows(colour, through):
    total = [v[0:1] for v in colour]
    front = through[0:1]
    for s in range(1, 8):
        total = [t + front * v[s : s + 1] for t, v in zip(total, colour)]
        front = front * through[s : s + 1]
    return total + [front]


def add_cell(state, passed, emission):
    red, green, blue, through = state
    weight = through * (1.0 - passed)
    return (
        red + weight * emission[0],
        green + weight * emission[1],
        blue + weight * emission[2],
        through * passed,
    )


def start_state():
    zero = jnp.zeros((8, 128), jnp.float32)
    return (zero, zero, zero, jnp.ones((8, 128), jnp.float32))


def yz_kernel(step, field_ref, mark_ref, transfer_ref, gain_ref, y_ref, z_ref, tables_ref, cell_ref, turned_ref):
    tile = pl.program_id(1)

    @pl.when((pl.program_id(0) == 0) & (tile == 0))
    def _():
        make_tables(transfer_ref, tables_ref)

    tables = [tables_ref[k] for k in range(6)]
    rows = field_ref.shape[1]
    run = rows // 8

    def along_y(j, state):
        at = pl.ds(j, 8, stride=run)
        red, green, blue, extinction = classify(field_ref[0, at, :], mark_ref[0, at, :], tables, gain_ref)
        passed = jnp.exp(extinction * -step)
        for c, v in enumerate((red, green, blue, passed)):
            cell_ref[c, at, :] = v
        return add_cell(state, passed, (red, green, blue))

    state = lax.fori_loop(0, run, along_y, start_state(), unroll=16)
    for c, v in enumerate(join_rows(state[:3], state[3])):
        y_ref[0, c, :] = v[0]

    to = pl.ds(pl.multiple_of(tile * 128, 128), 128)
    for c in range(4):
        for k in range(rows // 128):
            turned_ref[c, k, to, :] = cell_ref[c, pl.ds(k * 128, 128), :].T

    @pl.when(tile == pl.num_programs(1) - 1)
    def _():
        length = turned_ref.shape[2]
        run = length // 8
        for k in range(turned_ref.shape[1]):

            def along_z(j, state):
                at = pl.ds(j, 8, stride=run)
                red, green, blue, passed = [turned_ref[c, k, at, :] for c in range(4)]
                return add_cell(state, passed, (red, green, blue))

            state = lax.fori_loop(0, run, along_z, start_state(), unroll=8)
            for c, v in enumerate(join_rows(state[:3], state[3])):
                z_ref[0, c, pl.ds(k * 128, 128)] = v[0]


def yz_views(field, marks, transfer_table, material_gain, step):
    depth, rows, cols = field.shape
    block = pl.BlockSpec((1, rows, 128), lambda i, j: (i, 0, j))
    return pl.pallas_call(
        functools.partial(yz_kernel, step),
        grid=(depth, cols // 128),
        in_specs=[
            block,
            block,
            pl.BlockSpec(transfer_table.shape, lambda i, j: (0, 0)),
            pl.BlockSpec(memory_space=pltpu.SMEM),
        ],
        out_specs=[
            pl.BlockSpec((1, 4, 128), lambda i, j: (i, 0, j)),
            pl.BlockSpec((1, 4, rows), lambda i, j: (i, 0, 0)),
        ],
        out_shape=[
            jax.ShapeDtypeStruct((depth, 4, cols), jnp.float32),
            jax.ShapeDtypeStruct((depth, 4, rows), jnp.float32),
        ],
        scratch_shapes=[
            pltpu.VMEM((6, 8, 128), jnp.int32),
            pltpu.VMEM((4, rows, 128), jnp.float32),
            pltpu.VMEM((4, rows // 128, cols, 128), jnp.float32),
        ],
        name="yz_views",
    )(field, marks, transfer_table, material_gain)


def x_frame_kernel(order_ref, part_ref, out_ref):
    slabs = part_ref.shape[0]
    first = part_ref.at[order_ref[0]]
    total = [first[c] for c in range(3)]
    front = first[3]
    for k in range(1, slabs):
        part = part_ref.at[order_ref[k]]
        total = [t + front * part[c] for c, t in enumerate(total)]
        front = front * part[3]
    for c, v in enumerate(total + [front]):
        out_ref[c] = v


def x_frame(parts, order):
    return pl.pallas_call(
        x_frame_kernel,
        in_specs=[pl.BlockSpec(memory_space=pltpu.SMEM), pl.BlockSpec(memory_space=pltpu.VMEM)],
        out_specs=pl.BlockSpec(memory_space=pltpu.VMEM),
        out_shape=jax.ShapeDtypeStruct(parts.shape[1:], jnp.float32),
        compiler_params=pltpu.CompilerParams(vmem_limit_bytes=8 << 20),
        name="x_frame",
    )(order, parts)


def yz_frame_kernel(y_order_ref, z_order_ref, y_part_ref, z_part_ref, y_out_ref, z_out_ref):
    for order_ref, part_ref, out_ref in (
        (y_order_ref, y_part_ref, y_out_ref),
        (z_order_ref, z_part_ref, z_out_ref),
    ):
        slabs, depth, _, cols = part_ref.shape
        for x in range(depth):
            first = part_ref.at[order_ref[0], x]
            total = [first[pl.ds(c, 1), :] for c in range(3)]
            front = first[pl.ds(3, 1), :]
            for k in range(1, slabs):
                part = part_ref.at[order_ref[k], x]
                total = [t + front * part[pl.ds(c, 1), :] for c, t in enumerate(total)]
                front = front * part[pl.ds(3, 1), :]
            for c, v in enumerate(total + [front]):
                out_ref[c, pl.ds(x, 1), :] = v


def yz_frames(y_parts, z_parts, y_order, z_order):
    smem = pl.BlockSpec(memory_space=pltpu.SMEM)
    vmem = pl.BlockSpec(memory_space=pltpu.VMEM)
    shape = lambda parts: jax.ShapeDtypeStruct((4, parts.shape[1], parts.shape[3]), jnp.float32)
    return pl.pallas_call(
        yz_frame_kernel,
        in_specs=[smem, smem, vmem, vmem],
        out_specs=[vmem, vmem],
        out_shape=[shape(y_parts), shape(z_parts)],
        name="yz_frames",
    )(y_order, z_order, y_parts, z_parts)


def shards(scalar_field, materials, transfer_table, material_gain, depth_order_x, depth_order_y, depth_order_z):
    cells_x, cells_y, cells_z = scalar_field.shape
    pieces = lax.axis_size("gx")
    step_x = 1.0 / (cells_x * pieces)
    step_y = 1.0 / (cells_y * lax.axis_size("gy"))
    step_z = 1.0 / (cells_z * lax.axis_size("gz"))
    assert step_y == step_z
    image_x = x_view(scalar_field, materials, transfer_table, material_gain, step_x, pieces)
    parts_x = lax.all_to_all(image_x, "gx", split_axis=0, concat_axis=0, tiled=True)
    image_y, image_z = yz_views(scalar_field, materials, transfer_table, material_gain, step_y)
    parts_y = lax.all_gather(image_y, "gy", axis=0)
    parts_z = lax.all_gather(image_z, "gz", axis=0)
    frame_y, frame_z = yz_frames(parts_y, parts_z, depth_order_y, depth_order_z)
    tile_order = depth_order_x[lax.axis_index("gy"), lax.axis_index("gz")]
    frame_x = x_frame(parts_x, tile_order)
    return frame_x[:, None, None], frame_y, frame_z


def solution(mesh):
    return jax.shard_map(
        shards,
        mesh=mesh,
        in_specs=(P("gx", "gy", "gz"), P("gx", "gy", "gz"), P(), P(), P(), P(), P()),
        out_specs=(P(None, "gy", "gx", None, "gz"), P(None, "gx", "gz"), P(None, "gx", "gy")),
        check_vma=False,
    )
```

```python
import functools
import jax
import jax.numpy as jnp
from jax import lax
from jax.experimental import pallas as pl
from jax.experimental.pallas import tpu as pltpu
from jax.sharding import PartitionSpec as P


LOG2_E = 1.4426950408889634


def look_up(table, index):
    return jnp.take_along_axis(table, index, axis=1, mode="promise_in_bounds")


def make_tables(transfer_ref, tables_ref):
    bins = transfer_ref.shape[1]
    lane = lax.broadcasted_iota(jnp.int32, (8, 128), 1)
    values, steps = [], []
    for c in range(4):
        value = jnp.broadcast_to(transfer_ref[pl.ds(c, 1), :], (8, bins))
        step = jnp.where(lane == bins - 1, 0.0, pltpu.roll(value, bins - 1, 1) - value)
        values.append((value * float(1 << 19) - 0.5).astype(jnp.int32) << 10)
        steps.append((step * float(1 << 18) + 1048576.0).astype(jnp.int32) - 1048576)
    for c in (2, 3):
        tables_ref[c + 1] = values[c]
        tables_ref[c + 3] = steps[c] << 11
    for pair in range(1):
        first, second = 2 * pair, 2 * pair + 1
        tables_ref[3 * pair] = values[first] | (steps[second] & 1023)
        tables_ref[3 * pair + 1] = values[second] | 512
        tables_ref[3 * pair + 2] = (steps[first] << 11) | ((steps[second] >> 10) & 2047)


def classify(cells, marks, tables, gain_ref, extinction_scale=1.0):
    scaled = cells * (tables[0].shape[1] - 1.0)
    lower = scaled.astype(jnp.int32)
    fraction = scaled - lower.astype(jnp.float32)
    words = [look_up(table, lower) for table in tables]
    samples = []
    for pair in range(1):
        first, second, step = words[3 * pair : 3 * pair + 3]
        samples.append(first.astype(jnp.float32) + fraction * step.astype(jnp.float32))
        step = (step << 21) | ((first & 1023) << 11)
        samples.append(second.astype(jnp.float32) + fraction * step.astype(jnp.float32))
    for value, step in zip(words[3:5], words[5:7]):
        samples.append(value.astype(jnp.float32) + fraction * step.astype(jnp.float32))
    bits = [marks & (1 << k) != 0 for k in range((gain_ref.shape[1] - 1).bit_length())]
    out = []
    for c in range(4):
        scale = (extinction_scale if c == 3 else 1.0) / (1 << 29)
        gains = [gain_ref[c, k] * scale for k in range(gain_ref.shape[1])]
        for bit in bits:
            gains = [jnp.where(bit, high, low) for low, high in zip(gains[0::2], gains[1::2])]
        out.append(samples[c] * gains[0])
    return out


def x_kernel(step, field_ref, mark_ref, transfer_ref, gain_ref, out_ref, tables_ref):
    @pl.when(pl.program_id(0) == 0)
    def _():
        make_tables(transfer_ref, tables_ref)

    tables = [tables_ref[k] for k in range(7)]
    depth, rows, cols = field_ref.shape
    piece_rows = out_ref.shape[2]
    for piece in range(out_ref.shape[0]):
        for col in range(0, cols, 128):
            for row in range(0, piece_rows, 8):
                colour = None
                for x in range(depth):
                    at = (x, pl.ds(piece * piece_rows + row, 8), pl.ds(col, 128))
                    red, green, blue, extinction = classify(field_ref[at], mark_ref[at], tables, gain_ref, -step * LOG2_E)
                    passed = jnp.exp2(extinction)
                    if colour is None:
                        weight = 1.0 - passed
                        colour = [weight * v for v in (red, green, blue)]
                        through = passed
                    else:
                        after = through * passed
                        weight = through - after
                        colour = [a + weight * v for a, v in zip(colour, (red, green, blue))]
                        through = after
                for c, v in enumerate(colour + [through]):
                    out_ref[piece, c, pl.ds(row, 8), pl.ds(col, 128)] = v


def x_view(field, marks, transfer_table, material_gain, step, pieces, per_step=4):
    depth, rows, cols = field.shape
    piece_rows = rows // pieces
    block = pl.BlockSpec((depth, per_step * piece_rows, cols), lambda i: (0, i, 0))
    return pl.pallas_call(
        functools.partial(x_kernel, step),
        grid=(pieces // per_step,),
        in_specs=[
            block,
            block,
            pl.BlockSpec(transfer_table.shape, lambda i: (0, 0)),
            pl.BlockSpec(memory_space=pltpu.SMEM),
        ],
        out_specs=pl.BlockSpec((per_step, 4, piece_rows, cols), lambda i: (i, 0, 0, 0)),
        out_shape=jax.ShapeDtypeStruct((pieces, 4, piece_rows, cols), jnp.float32),
        scratch_shapes=[pltpu.VMEM((7, 8, 128), jnp.int32)],
        name="x_view",
    )(field, marks, transfer_table, material_gain)


def join_rows(colour, through):
    total = [v[0:1] for v in colour]
    front = through[0:1]
    for s in range(1, 8):
        total = [t + front * v[s : s + 1] for t, v in zip(total, colour)]
        front = front * through[s : s + 1]
    return total + [front]


def add_cell(state, passed, emission):
    red, green, blue, through = state
    weight = through * (1.0 - passed)
    return (
        red + weight * emission[0],
        green + weight * emission[1],
        blue + weight * emission[2],
        through * passed,
    )


def start_state():
    zero = jnp.zeros((8, 128), jnp.float32)
    return (zero, zero, zero, jnp.ones((8, 128), jnp.float32))


def yz_kernel(step, field_ref, mark_ref, transfer_ref, gain_ref, y_ref, z_ref, tables_ref, cell_ref, turned_ref):
    tile = pl.program_id(1)

    @pl.when((pl.program_id(0) == 0) & (tile == 0))
    def _():
        make_tables(transfer_ref, tables_ref)

    tables = [tables_ref[k] for k in range(7)]
    rows = field_ref.shape[1]
    run = rows // 8

    def along_y(j, state):
        at = pl.ds(j, 8, stride=run)
        red, green, blue, extinction = classify(field_ref[0, at, :], mark_ref[0, at, :], tables, gain_ref)
        passed = jnp.exp(extinction * -step)
        for c, v in enumerate((red, green, blue, passed)):
            cell_ref[c, at, :] = v
        return add_cell(state, passed, (red, green, blue))

    state = lax.fori_loop(0, run, along_y, start_state(), unroll=16)
    for c, v in enumerate(join_rows(state[:3], state[3])):
        y_ref[0, c, :] = v[0]

    to = pl.ds(pl.multiple_of(tile * 128, 128), 128)
    for c in range(4):
        for k in range(rows // 128):
            turned_ref[c, k, to, :] = cell_ref[c, pl.ds(k * 128, 128), :].T

    @pl.when(tile == pl.num_programs(1) - 1)
    def _():
        length = turned_ref.shape[2]
        run = length // 8
        for k in range(turned_ref.shape[1]):

            def along_z(j, state):
                at = pl.ds(j, 8, stride=run)
                red, green, blue, passed = [turned_ref[c, k, at, :] for c in range(4)]
                return add_cell(state, passed, (red, green, blue))

            state = lax.fori_loop(0, run, along_z, start_state(), unroll=8)
            for c, v in enumerate(join_rows(state[:3], state[3])):
                z_ref[0, c, pl.ds(k * 128, 128)] = v[0]


def yz_views(field, marks, transfer_table, material_gain, step):
    depth, rows, cols = field.shape
    block = pl.BlockSpec((1, rows, 128), lambda i, j: (i, 0, j))
    return pl.pallas_call(
        functools.partial(yz_kernel, step),
        grid=(depth, cols // 128),
        in_specs=[
            block,
            block,
            pl.BlockSpec(transfer_table.shape, lambda i, j: (0, 0)),
            pl.BlockSpec(memory_space=pltpu.SMEM),
        ],
        out_specs=[
            pl.BlockSpec((1, 4, 128), lambda i, j: (i, 0, j)),
            pl.BlockSpec((1, 4, rows), lambda i, j: (i, 0, 0)),
        ],
        out_shape=[
            jax.ShapeDtypeStruct((depth, 4, cols), jnp.float32),
            jax.ShapeDtypeStruct((depth, 4, rows), jnp.float32),
        ],
        scratch_shapes=[
            pltpu.VMEM((7, 8, 128), jnp.int32),
            pltpu.VMEM((4, rows, 128), jnp.float32),
            pltpu.VMEM((4, rows // 128, cols, 128), jnp.float32),
        ],
        name="yz_views",
    )(field, marks, transfer_table, material_gain)


def x_frame_kernel(order_ref, part_ref, out_ref):
    slabs = part_ref.shape[0]
    first = part_ref.at[order_ref[0]]
    total = [first[c] for c in range(3)]
    front = first[3]
    for k in range(1, slabs):
        part = part_ref.at[order_ref[k]]
        total = [t + front * part[c] for c, t in enumerate(total)]
        front = front * part[3]
    for c, v in enumerate(total + [front]):
        out_ref[c] = v


def x_frame(parts, order):
    return pl.pallas_call(
        x_frame_kernel,
        in_specs=[pl.BlockSpec(memory_space=pltpu.SMEM), pl.BlockSpec(memory_space=pltpu.VMEM)],
        out_specs=pl.BlockSpec(memory_space=pltpu.VMEM),
        out_shape=jax.ShapeDtypeStruct(parts.shape[1:], jnp.float32),
        compiler_params=pltpu.CompilerParams(vmem_limit_bytes=8 << 20),
        name="x_frame",
    )(order, parts)


def yz_frame_kernel(y_order_ref, z_order_ref, y_part_ref, z_part_ref, y_out_ref, z_out_ref):
    for order_ref, part_ref, out_ref in (
        (y_order_ref, y_part_ref, y_out_ref),
        (z_order_ref, z_part_ref, z_out_ref),
    ):
        slabs, depth, _, cols = part_ref.shape
        for x in range(depth):
            first = part_ref.at[order_ref[0], x]
            total = [first[pl.ds(c, 1), :] for c in range(3)]
            front = first[pl.ds(3, 1), :]
            for k in range(1, slabs):
                part = part_ref.at[order_ref[k], x]
                total = [t + front * part[pl.ds(c, 1), :] for c, t in enumerate(total)]
                front = front * part[pl.ds(3, 1), :]
            for c, v in enumerate(total + [front]):
                out_ref[c, pl.ds(x, 1), :] = v


def yz_frames(y_parts, z_parts, y_order, z_order):
    smem = pl.BlockSpec(memory_space=pltpu.SMEM)
    vmem = pl.BlockSpec(memory_space=pltpu.VMEM)
    shape = lambda parts: jax.ShapeDtypeStruct((4, parts.shape[1], parts.shape[3]), jnp.float32)
    return pl.pallas_call(
        yz_frame_kernel,
        in_specs=[smem, smem, vmem, vmem],
        out_specs=[vmem, vmem],
        out_shape=[shape(y_parts), shape(z_parts)],
        name="yz_frames",
    )(y_order, z_order, y_parts, z_parts)


def shards(scalar_field, materials, transfer_table, material_gain, depth_order_x, depth_order_y, depth_order_z):
    cells_x, cells_y, cells_z = scalar_field.shape
    pieces = lax.axis_size("gx")
    step_x = 1.0 / (cells_x * pieces)
    step_y = 1.0 / (cells_y * lax.axis_size("gy"))
    step_z = 1.0 / (cells_z * lax.axis_size("gz"))
    assert step_y == step_z
    image_x = x_view(scalar_field, materials, transfer_table, material_gain, step_x, pieces)
    parts_x = lax.all_to_all(image_x, "gx", split_axis=0, concat_axis=0, tiled=True)
    image_y, image_z = yz_views(scalar_field, materials, transfer_table, material_gain, step_y)
    parts_y = lax.all_gather(image_y, "gy", axis=0)
    parts_z = lax.all_gather(image_z, "gz", axis=0)
    frame_y, frame_z = yz_frames(parts_y, parts_z, depth_order_y, depth_order_z)
    tile_order = depth_order_x[lax.axis_index("gy"), lax.axis_index("gz")]
    frame_x = x_frame(parts_x, tile_order)
    return frame_x[:, None, None], frame_y, frame_z


def solution(mesh):
    return jax.shard_map(
        shards,
        mesh=mesh,
        in_specs=(P("gx", "gy", "gz"), P("gx", "gy", "gz"), P(), P(), P(), P(), P()),
        out_specs=(P(None, "gy", "gx", None, "gz"), P(None, "gx", "gz"), P(None, "gx", "gy")),
        check_vma=False,
    )
```
